1024 devices in a mesh: loop: 32 (over y_lo, z, core), layer: 32 (over y_hi, x).
Axes of the slice: x: 8, y: 8 (y_hi: 4, y_lo: 2; y = y_hi * 2 + y_lo), z: 8, core: 2. Of those that a mesh axis runs over, the one named last changes fastest.
Arguments:
- flow_cols: bfloat16 [262144, 256], P(('loop', 'layer')), may hold values from -6 to 6
- restart: bfloat16 [262144, 256], P(('loop', 'layer')), may hold values from -6 to 6
- tile_blocks: bfloat16 [24576, 256, 256], P(('loop', 'layer')), may hold values from -0.078125 to 0.078125
- tile_rows: int32 [24576], P(('loop', 'layer')), may hold values from 0 to 31
- tile_srcs: int32 [24576], P(('loop', 'layer')), may hold values from 0 to 31, as said below
- tile_count: int32 [1024], P(('loop', 'layer')), may hold values from 16 to 24, as said below
- dangling: int32 [262144], P(('loop', 'layer')), may hold values 0 or 1
Outputs:
- next_flow: bfloat16 [262144, 256], P(('loop', 'layer'))
The draws below stay inside these ranges and needn't reach their ends.
Inputs may be any that keep to these rules, and one draw needn't show every extreme that they name: `tile_srcs`: within each device's aligned block of 24 slots the source row blocks never fall. `tile_count`: slots at or beyond a device's count hold no tile; some device uses all 24 slots.
All inputs are finite; a program needn't handle non-finite values. No bound on the sum of `dangling` on one device may be relied on, other than what follows from the above.
Results may differ from the reference program's by a relative error of at most 0.017.
Values may be sent and summed in bfloat16 or wider, within the bound.
No kernel may reach another device: no remote copies, remote signals or barrier semaphores. Data moves between devices by JAX's collectives and lax.ppermute only.
A program may use at most 64 MiB of HBM per device.

```python
import jax
import jax.numpy as jnp
from jax import lax

TILE = 256
FLOWS = 256
MAXT = 24
DEVS = 1024
NODES = 262144
N_LOOP = 32
N_LAYER = 32


def draw_tile_srcs(key, part):
    values = jax.random.randint(key, (DEVS, MAXT), 0, N_LOOP)
    return jnp.sort(values, axis=1).reshape(-1).astype(jnp.int32)


def draw_tile_count(key, part):
    lowest = max(1, 2 * MAXT // 3)
    counts = jax.random.randint(jax.random.fold_in(key, 11), (DEVS,), lowest, MAXT + 1)
    chosen = jax.random.randint(jax.random.fold_in(key, 12), (), 0, DEVS)
    counts = counts.at[chosen].set(MAXT)
    return counts.astype(jnp.int32)


def with_ends(entries, key, low, high):
    longest = entries.shape.index(max(entries.shape))
    spots = []
    for shift in (0, 1):
        where = [jax.random.randint(jax.random.fold_in(key, axis), (), 0, length) for axis, length in enumerate(entries.shape)]
        where[longest] = (where[longest] + shift) % entries.shape[longest]
        spots.append(tuple(where))
    return entries.at[spots[0]].set(low).at[spots[1]].set(high)


def steps_of(rng, shape, shards, smallest, top_value):
    gain, own = 1.0, jax.random.fold_in(rng, 6)
    for position, blocks in shards:
        draws = jnp.exp(jax.random.uniform(jax.random.fold_in(own, position), (blocks,), jnp.float32, smallest / len(shards), top_value / len(shards)))
        gain = gain * jnp.repeat(draws, shape[position] // blocks).reshape([-1 if axis == position else 1 for axis in range(len(shape))])
    return gain


def noise(key, shape, spread, limit, split=(), kind=jnp.bfloat16):
    array = spread * jax.random.normal(key, shape, jnp.float32)
    if split:
        array = array * steps_of(key, shape, split, -0.22, 0.18)
    return jnp.clip(array, -limit, limit).astype(kind)


def setup_inputs(seed: int = 0) -> dict:
    key_list = jax.random.split(jax.random.key(seed), 8)
    flow_cols = noise(key_list[0], (NODES, FLOWS), 1.0, 6.0, ((0, 1024),))
    restart = noise(key_list[1], (NODES, FLOWS), 1.0, 6.0, ((0, 1024),))
    tile_blocks = noise(key_list[2], (DEVS * MAXT, TILE, TILE), (TILE * MAXT) ** -0.5, 0.078125, ((0, 1024),))
    tile_rows = with_ends(jax.random.randint(key_list[3], (DEVS * MAXT,), 0, N_LAYER), jax.random.fold_in(key_list[3], 1), 0, N_LAYER - 1).astype(jnp.int32)
    tile_srcs = draw_tile_srcs(jax.random.fold_in(key_list[7], 71), 0)
    tile_count = draw_tile_count(jax.random.fold_in(key_list[7], 71), 0)
    dangling = with_ends((jax.random.randint(key_list[6], (NODES,), 0, 4) < 1).astype(jnp.int32), jax.random.fold_in(key_list[6], 1), 0, 1)
    return dict(flow_cols=flow_cols, restart=restart, tile_blocks=tile_blocks, tile_rows=tile_rows, tile_srcs=tile_srcs, tile_count=tile_count, dangling=dangling)


DAMP = 0.85


def reference(flow_cols, restart, tile_blocks, tile_rows, tile_srcs, tile_count, dangling):
    columns = flow_cols.shape[1]
    block_rows = N_LAYER * TILE

    def per_device(running, device):
        loop_id = device // N_LAYER
        layer_id = device % N_LAYER
        used_tiles = tile_count[device]

        def per_tile(current, slot_index):
            entry = device * MAXT + slot_index

            def add_tile(held):
                src_start = ((tile_srcs[entry] * N_LAYER + layer_id) * TILE).astype(jnp.int32)
                source_panel = lax.dynamic_slice_in_dim(flow_cols, src_start, TILE, 0)
                tile_block = lax.dynamic_index_in_dim(tile_blocks, entry, 0, keepdims=False)
                product = jnp.dot(tile_block, source_panel, preferred_element_type=jnp.float32)
                row_start = (tile_rows[entry] * TILE).astype(jnp.int32)
                earlier = lax.dynamic_slice_in_dim(held, row_start, TILE, 0)
                return lax.dynamic_update_slice_in_dim(held, earlier + product, row_start, 0)

            def keep_same(held):
                return held

            return lax.cond(slot_index < used_tiles, add_tile, keep_same, current), None

        partial_value, unused = lax.scan(per_tile, jnp.zeros((block_rows, columns), jnp.float32),
                                   jnp.arange(MAXT, dtype=jnp.int32))
        rounded = lax.optimization_barrier(partial_value.astype(jnp.bfloat16))
        partial_value = rounded.astype(jnp.float32)
        block_start = (loop_id * block_rows).astype(jnp.int32)
        earlier = lax.dynamic_slice_in_dim(running, block_start, block_rows, 0)
        return lax.dynamic_update_slice_in_dim(running, earlier + partial_value, block_start, 0), None

    propagated, unused = lax.scan(per_device, jnp.zeros(flow_cols.shape, jnp.float32),
                                  jnp.arange(N_LOOP * N_LAYER, dtype=jnp.int32))
    own_flow = flow_cols.astype(jnp.float32)
    mask_col = dangling.astype(jnp.float32)[:, None]
    result = DAMP * (propagated + mask_col * own_flow) + (1.0 - DAMP) * restart.astype(jnp.float32)
    return result.astype(jnp.bfloat16)
```

```python
import jax
import jax.numpy as jnp
from jax import lax
from jax.experimental import pallas as pl
from jax.experimental.pallas import tpu as pltpu
from jax.sharding import Mesh, PartitionSpec as P

DAMP = 0.85
LOOP = (("ylo", 2), ("z", 8), ("core", 2))
LAYER = (("yhi", 4), ("x", 8))
LOOP_AXES = tuple(name for name, _ in LOOP)
LAYER_AXES = tuple(name for name, _ in LAYER)
N_YHI, N_X = 4, 8
ROW_TILES = N_YHI * N_X


def tiles_kernel(count, rows, srcs, tiles, panels, out, head, following, acc):
    side = tiles.shape[1]

    def clear(r, carry):
        head[r] = -1
        return carry

    lax.fori_loop(0, ROW_TILES, clear, 0)

    def link(s, carry):
        r = rows[s]
        following[s] = head[r]
        head[r] = s
        return carry

    lax.fori_loop(0, count[0], link, 0)

    def block(p, carry):
        r = (p % N_YHI) * N_X + p // N_YHI
        first = head[r]
        where = pl.ds(pl.multiple_of(p * side, side), side)

        @pl.when(first < 0)
        def _():
            out[where, :] = jnp.zeros((side, out.shape[1]), out.dtype)

        @pl.when(first >= 0)
        def _():
            def product(s):
                source = pl.ds(pl.multiple_of(srcs[s] * side, side), side)
                return jnp.dot(tiles[s], panels[source, :], preferred_element_type=jnp.float32)

            acc[...] = product(first)

            def more(s):
                acc[...] += product(s)
                return following[s]

            lax.while_loop(lambda s: s >= 0, more, following[first])
            out[where, :] = acc[...].astype(out.dtype)

        return carry

    lax.fori_loop(0, ROW_TILES, block, 0)


def partial_products(tile_blocks, tile_rows, tile_srcs, tile_count, panels):
    slots, side = tile_blocks.shape[:2]
    columns = panels.shape[1]
    smem = pl.BlockSpec(memory_space=pltpu.SMEM)
    vmem = pl.BlockSpec(memory_space=pltpu.VMEM)
    return pl.pallas_call(
        tiles_kernel,
        out_shape=jax.ShapeDtypeStruct((ROW_TILES * side, columns), jnp.bfloat16),
        in_specs=[smem, smem, smem, vmem, vmem],
        out_specs=vmem,
        scratch_shapes=[
            pltpu.SMEM((ROW_TILES,), jnp.int32),
            pltpu.SMEM((slots,), jnp.int32),
            pltpu.VMEM((side, columns), jnp.float32),
        ],
        compiler_params=pltpu.CompilerParams(vmem_limit_bytes=40 << 20),
        name="tile_products",
    )(tile_count, tile_rows, tile_srcs, tile_blocks, panels)


def body(flow_cols, restart, tile_blocks, tile_rows, tile_srcs, tile_count, dangling):
    side, columns = flow_cols.shape
    panels = lax.all_gather(flow_cols, LOOP_AXES, axis=0, tiled=True)
    partial = partial_products(tile_blocks, tile_rows, tile_srcs, tile_count, panels)
    along_x = lax.psum_scatter(partial, "x", scatter_dimension=0, tiled=True)
    shares = lax.all_to_all(along_x.reshape(N_YHI, side, columns), "yhi", 0, 0)
    summed = jnp.sum(shares.astype(jnp.float32), axis=0)
    own_flow = flow_cols.astype(jnp.float32)
    mask_col = dangling.astype(jnp.float32)[:, None]
    result = DAMP * (summed + mask_col * own_flow) + (1.0 - DAMP) * restart.astype(jnp.float32)
    return result.astype(jnp.bfloat16)


def solution(mesh):
    names = LOOP_AXES + LAYER_AXES
    sizes = [size for _, size in LOOP + LAYER]
    fine = Mesh(mesh.devices.reshape(sizes), names)
    rows = P(names, None)
    in_specs = (rows, rows, P(names, None, None), P(names), P(names), P(names), P(names))
    return jax.shard_map(body, mesh=fine, in_specs=in_specs, out_specs=rows, check_vma=False)
```

```python
import jax
import jax.numpy as jnp
from jax import lax
from jax.experimental import pallas as pl
from jax.experimental.pallas import tpu as pltpu
from jax.sharding import Mesh, PartitionSpec as P

DAMP = 0.85
LOOP = (("ylo", 2), ("z", 8), ("core", 2))
LAYER = (("yhi", 4), ("x", 8))
SIZES = dict(LOOP + LAYER)
N_YLO, N_Z, N_CORE = SIZES["ylo"], SIZES["z"], SIZES["core"]
N_YHI, N_X = SIZES["yhi"], SIZES["x"]
ROW_TILES = N_YHI * N_X


def shifted(value, axis, by):
    size = SIZES[axis]
    return lax.ppermute(value, axis, [(i, (i + by) % size) for i in range(size)])


def tiles_kernel(
    count, rows, srcs, tiles, near, across, far_up, far_down, rest, head, following, acc
):
    side = tiles.shape[1]
    my_ylo, my_z, my_core = lax.axis_index("ylo"), lax.axis_index("z"), lax.axis_index("core")
    my_x = lax.axis_index("x")

    def clear(r, carry):
        head[r] = -1
        return carry

    lax.fori_loop(0, ROW_TILES, clear, 0)

    def link(s, carry):
        r = rows[s]
        following[s] = head[r]
        head[r] = s
        return carry

    lax.fori_loop(0, count[0], link, 0)

    def add_product(s):
        src = srcs[s]
        dz = ((src // N_CORE) % N_Z + N_Z - my_z) % N_Z
        dy = (src // (N_CORE * N_Z) + N_YLO - my_ylo) % N_YLO
        slot = jnp.where(dz >= N_Z // 2, (N_Z - dz) * 2 - 1, 2 * dz)
        panel = pl.ds(pl.multiple_of((slot * N_YLO + dy) * side, side), side)
        same_core = src % N_CORE == my_core

        @pl.when(same_core)
        def _():
            acc[...] += jnp.dot(tiles[s], near[panel, :], preferred_element_type=jnp.float32)

        @pl.when(jnp.logical_not(same_core))
        def _():
            acc[...] += jnp.dot(tiles[s], across[panel, :], preferred_element_type=jnp.float32)

        return following[s]

    def fill(out, blocks, row_of):
        def block(p, carry):
            first = head[row_of(p)]
            where = pl.ds(pl.multiple_of(p * side, side), side)

            @pl.when(first < 0)
            def _():
                out[where, :] = jnp.zeros((side, out.shape[1]), out.dtype)

            @pl.when(first >= 0)
            def _():
                acc[...] = jnp.zeros_like(acc)
                lax.while_loop(lambda s: s >= 0, add_product, first)
                out[where, :] = acc[...].astype(out.dtype)

            return carry

        lax.fori_loop(0, blocks, block, 0)

    def row(k, yhi):
        return yhi * N_X + (my_x + k) % N_X

    half = N_YHI // 2
    fill(far_up, half, lambda p: row(N_X // 2, p))
    fill(far_down, half, lambda p: row(N_X // 2, p + half))

    def rest_row(p):
        i = p // N_YHI
        k = jnp.where(i % 2 == 0, N_X // 2 - 1 - i // 2, N_X // 2 + 1 + i // 2)
        return row(k, p % N_YHI)

    fill(rest, (N_X - 1) * N_YHI, rest_row)


def partial_products(tile_blocks, tile_rows, tile_srcs, tile_count, near, across):
    slots, side = tile_blocks.shape[:2]
    columns = near.shape[1]
    smem = pl.BlockSpec(memory_space=pltpu.SMEM)
    vmem = pl.BlockSpec(memory_space=pltpu.VMEM)

    def out(tiles):
        return jax.ShapeDtypeStruct((tiles * side, columns), jnp.bfloat16)

    return pl.pallas_call(
        tiles_kernel,
        out_shape=(out(N_YHI // 2), out(N_YHI // 2), out((N_X - 1) * N_YHI)),
        in_specs=[smem, smem, smem, vmem, vmem, vmem],
        out_specs=(vmem, vmem, vmem),
        scratch_shapes=[
            pltpu.SMEM((ROW_TILES,), jnp.int32),
            pltpu.SMEM((slots,), jnp.int32),
            pltpu.VMEM((side, columns), jnp.float32),
        ],
        compiler_params=pltpu.CompilerParams(vmem_limit_bytes=24 << 20),
        name="tile_products",
    )(tile_count, tile_rows, tile_srcs, tile_blocks, near, across)


def gather_panels(flow_cols):
    side = flow_cols.shape[0]
    own = jnp.concatenate([flow_cols, shifted(flow_cols, "ylo", 1)], 0)
    below1, above1 = shifted(own, "z", 1), shifted(own, "z", -1)
    below2, above2 = shifted(own, "z", 2), shifted(own, "z", -2)
    below3, above3 = shifted(below2, "z", 1), shifted(above2, "z", -1)
    below4, above4 = shifted(below2[:side], "z", 2), shifted(above2[side:], "z", -2)
    near = jnp.concatenate(
        [own, below1, above1, below2, above2, below3, above3, below4, above4], 0
    )
    return near, shifted(near, "core", 1)


def add(*terms):
    total = terms[0].astype(jnp.float32)
    for term in terms[1:]:
        total = total + term.astype(jnp.float32)
    return total.astype(jnp.bfloat16)


def reduce_along_x(far_up, far_down, rest):
    chunk = 2 * far_up.shape[0]
    half = far_up.shape[0]
    up3, down3, up2, down2, up1, down1, own = (
        rest[i * chunk : (i + 1) * chunk] for i in range(N_X - 1)
    )
    up, down = shifted(far_up, "x", 1), shifted(far_down, "x", -1)
    up = shifted(jnp.concatenate([add(up3[:half], up), up3[half:]], 0), "x", 1)
    down = shifted(jnp.concatenate([down3[:half], add(down3[half:], down)], 0), "x", -1)
    up, down = shifted(add(up2, up), "x", 1), shifted(add(down2, down), "x", -1)
    up, down = shifted(add(up1, up), "x", 1), shifted(add(down1, down), "x", -1)
    return add(own, up, down)


def body(flow_cols, restart, tile_blocks, tile_rows, tile_srcs, tile_count, dangling):
    side, columns = flow_cols.shape
    near, across = gather_panels(flow_cols)
    far_up, far_down, rest = partial_products(
        tile_blocks, tile_rows, tile_srcs, tile_count, near, across
    )
    along_x = reduce_along_x(far_up, far_down, rest)
    shares = lax.all_to_all(along_x.reshape(N_YHI, side, columns), "yhi", 0, 0)
    summed = jnp.sum(shares.astype(jnp.float32), axis=0)
    own_flow = flow_cols.astype(jnp.float32)
    mask_col = dangling.astype(jnp.float32)[:, None]
    result = DAMP * (summed + mask_col * own_flow) + (1.0 - DAMP) * restart.astype(jnp.float32)
    return result.astype(jnp.bfloat16)


def solution(mesh):
    names = tuple(SIZES)
    fine = Mesh(mesh.devices.reshape(tuple(SIZES.values())), names)
    rows = P(names, None)
    in_specs = (rows, rows, P(names, None, None), P(names), P(names), P(names), P(names))
    return jax.shard_map(body, mesh=fine, in_specs=in_specs, out_specs=rows, check_vma=False)
```

```python
import functools

import jax
import jax.numpy as jnp
from jax import lax
from jax.experimental import pallas as pl
from jax.experimental.pallas import tpu as pltpu
from jax.sharding import Mesh, PartitionSpec as P

DAMP = 0.85
LOOP = (("ylo", 2), ("z", 8), ("core", 2))
LAYER = (("yhi", 4), ("x", 8))
SIZES = dict(LOOP + LAYER)
N_YLO, N_Z, N_CORE = SIZES["ylo"], SIZES["z"], SIZES["core"]
N_YHI, N_X = SIZES["yhi"], SIZES["x"]
ROW_TILES = N_YHI * N_X


def shifted(value, axis, by):
    size = SIZES[axis]
    return lax.ppermute(value, axis, [(i, (i + by) % size) for i in range(size)])


def tiles_kernel(chunks, count, rows, srcs, tiles, near, across, *refs):
    outs, (head, following, acc) = refs[: len(chunks)], refs[len(chunks) :]
    side = tiles.shape[1]
    my_ylo, my_z, my_core = lax.axis_index("ylo"), lax.axis_index("z"), lax.axis_index("core")
    my_x = lax.axis_index("x")

    def clear(r, carry):
        head[r] = -1
        return carry

    lax.fori_loop(0, ROW_TILES, clear, 0)

    def link(s, carry):
        r = rows[s]
        following[s] = head[r]
        head[r] = s
        return carry

    lax.fori_loop(0, count[0], link, 0)

    def add_product(s):
        src = srcs[s]
        dz = ((src // N_CORE) % N_Z + N_Z - my_z) % N_Z
        dy = (src // (N_CORE * N_Z) + N_YLO - my_ylo) % N_YLO
        slot = jnp.where(dz >= N_Z // 2, (N_Z - dz) * 2 - 1, 2 * dz)
        panel = pl.ds(pl.multiple_of((slot * N_YLO + dy) * side, side), side)
        same_core = src % N_CORE == my_core

        @pl.when(same_core)
        def _():
            acc[...] += jnp.dot(tiles[s], near[panel, :], preferred_element_type=jnp.float32)

        @pl.when(jnp.logical_not(same_core))
        def _():
            acc[...] += jnp.dot(tiles[s], across[panel, :], preferred_element_type=jnp.float32)

        return following[s]

    for out, (k, yhis) in zip(outs, chunks):
        x = (my_x + k) % N_X

        def block(p, carry, out=out, x=x, yhis=yhis):
            first = head[(yhis.start + p) * N_X + x]
            where = pl.ds(pl.multiple_of(p * side, side), side)

            @pl.when(first < 0)
            def _():
                out[where, :] = jnp.zeros((side, out.shape[1]), out.dtype)

            @pl.when(first >= 0)
            def _():
                acc[...] = jnp.zeros_like(acc)
                lax.while_loop(lambda s: s >= 0, add_product, first)
                out[where, :] = acc[...].astype(out.dtype)

            return carry

        lax.fori_loop(0, len(yhis), block, 0)


def partial_products(chunks, tile_blocks, tile_rows, tile_srcs, tile_count, near, across):
    slots, side = tile_blocks.shape[:2]
    columns = near.shape[1]
    smem = pl.BlockSpec(memory_space=pltpu.SMEM)
    vmem = pl.BlockSpec(memory_space=pltpu.VMEM)
    row_tiles = sum(len(yhis) for _, yhis in chunks)
    return pl.pallas_call(
        functools.partial(tiles_kernel, chunks),
        out_shape=[
            jax.ShapeDtypeStruct((len(yhis) * side, columns), jnp.bfloat16) for _, yhis in chunks
        ],
        in_specs=[smem, smem, smem, vmem, vmem, vmem],
        out_specs=[vmem] * len(chunks),
        scratch_shapes=[
            pltpu.SMEM((ROW_TILES,), jnp.int32),
            pltpu.SMEM((slots,), jnp.int32),
            pltpu.VMEM((side, columns), jnp.float32),
        ],
        compiler_params=pltpu.CompilerParams(vmem_limit_bytes=24 << 20),
        cost_estimate=pl.CostEstimate(
            flops=2 * row_tiles * side * side * columns,
            transcendentals=0,
            bytes_accessed=4 * row_tiles * side * columns,
        ),
        name="tile_products",
    )(tile_count, tile_rows, tile_srcs, tile_blocks, near, across)


def gather_panels(flow_cols):
    side = flow_cols.shape[0]
    own = jnp.concatenate([flow_cols, shifted(flow_cols, "ylo", 1)], 0)
    below1, above1 = shifted(own, "z", 1), shifted(own, "z", -1)
    below2, above2 = shifted(own, "z", 2), shifted(own, "z", -2)
    below3, above3 = shifted(below2, "z", 1), shifted(above2, "z", -1)
    below4, above4 = shifted(below2[:side], "z", 2), shifted(above2[side:], "z", -2)
    near = jnp.concatenate(
        [own, below1, above1, below2, above2, below3, above3, below4, above4], 0
    )
    return near, shifted(near, "core", 1)


def add(*terms):
    total = terms[0].astype(jnp.float32)
    for term in terms[1:]:
        total = total + term.astype(jnp.float32)
    return total.astype(jnp.bfloat16)


def reduce_along_x(products):
    every, half = range(N_YHI), N_YHI // 2
    up4, down4, up3, down3 = products([(4, every[:half]), (4, every[half:]), (3, every), (5, every)])
    up2, down2, up1, down1, own = products([(k, every) for k in (2, 6, 1, 7, 0)])
    up, up_far = shifted(up3, "x", 1), shifted(up4, "x", 2)
    down, down_far = shifted(down3, "x", -1), shifted(down4, "x", -2)
    rows = up4.shape[0]
    up = jnp.concatenate([add(up2[:rows], up[:rows], up_far), add(up2[rows:], up[rows:])], 0)
    down = jnp.concatenate(
        [add(down2[:rows], down[:rows]), add(down2[rows:], down[rows:], down_far)], 0
    )
    up, down = shifted(up, "x", 1), shifted(down, "x", -1)
    up, down = shifted(add(up1, up), "x", 1), shifted(add(down1, down), "x", -1)
    return add(own, up, down)


def body(flow_cols, restart, tile_blocks, tile_rows, tile_srcs, tile_count, dangling):
    side, columns = flow_cols.shape
    near, across = gather_panels(flow_cols)

    def products(chunks):
        return partial_products(
            chunks, tile_blocks, tile_rows, tile_srcs, tile_count, near, across
        )

    along_x = reduce_along_x(products)
    shares = lax.all_to_all(along_x.reshape(N_YHI, side, columns), "yhi", 0, 0)
    summed = jnp.sum(shares.astype(jnp.float32), axis=0)
    own_flow = flow_cols.astype(jnp.float32)
    mask_col = dangling.astype(jnp.float32)[:, None]
    result = DAMP * (summed + mask_col * own_flow) + (1.0 - DAMP) * restart.astype(jnp.float32)
    return result.astype(jnp.bfloat16)


def solution(mesh):
    names = tuple(SIZES)
    fine = Mesh(mesh.devices.reshape(tuple(SIZES.values())), names)
    rows = P(names, None)
    in_specs = (rows, rows, P(names, None, None), P(names), P(names), P(names), P(names))
    return jax.shard_map(body, mesh=fine, in_specs=in_specs, out_specs=rows, check_vma=False)
```

```python
import functools

import jax
import jax.numpy as jnp
from jax import lax
from jax.experimental import pallas as pl
from jax.experimental.pallas import tpu as pltpu
from jax.sharding import Mesh, PartitionSpec as P

DAMP = 0.85
LOOP = (("ylo", 2), ("z", 8), ("core", 2))
LAYER = (("yhi", 4), ("x", 8))
SIZES = dict(LOOP + LAYER)
N_YLO, N_Z, N_CORE = SIZES["ylo"], SIZES["z"], SIZES["core"]
N_YHI, N_X = SIZES["yhi"], SIZES["x"]
ROW_TILES = N_YHI * N_X


def shifted(value, axis, by):
    size = SIZES[axis]
    return lax.ppermute(value, axis, [(i, (i + by) % size) for i in range(size)])


def tiles_kernel(chunks, count, rows, srcs, tiles, near, across, *refs):
    outs, (head, following, acc) = refs[: len(chunks)], refs[len(chunks) :]
    side = tiles.shape[1]
    my_ylo, my_z, my_core = lax.axis_index("ylo"), lax.axis_index("z"), lax.axis_index("core")
    my_x = lax.axis_index("x")

    def clear(r, carry):
        head[r] = -1
        return carry

    lax.fori_loop(0, ROW_TILES, clear, 0)

    def link(s, carry):
        r = rows[s]
        following[s] = head[r]
        head[r] = s
        return carry

    lax.fori_loop(0, count[0], link, 0)

    def add_product(s):
        src = srcs[s]
        dz = ((src // N_CORE) % N_Z + N_Z - my_z) % N_Z
        dy = (src // (N_CORE * N_Z) + N_YLO - my_ylo) % N_YLO
        slot = jnp.where(dz >= N_Z // 2, (N_Z - dz) * 2 - 1, 2 * dz)
        panel = pl.ds(pl.multiple_of((slot * N_YLO + dy) * side, side), side)
        same_core = src % N_CORE == my_core

        @pl.when(same_core)
        def _():
            acc[...] += jnp.dot(tiles[s], near[panel, :], preferred_element_type=jnp.float32)

        @pl.when(jnp.logical_not(same_core))
        def _():
            acc[...] += jnp.dot(tiles[s], across[panel, :], preferred_element_type=jnp.float32)

        return following[s]

    for out, (k, yhis) in zip(outs, chunks):
        x = (my_x + k) % N_X

        def block(p, carry, out=out, x=x, yhis=yhis):
            first = head[(yhis.start + p) * N_X + x]
            where = pl.ds(pl.multiple_of(p * side, side), side)

            @pl.when(first < 0)
            def _():
                out[where, :] = jnp.zeros((side, out.shape[1]), out.dtype)

            @pl.when(first >= 0)
            def _():
                acc[...] = jnp.zeros_like(acc)
                lax.while_loop(lambda s: s >= 0, add_product, first)
                out[where, :] = acc[...].astype(out.dtype)

            return carry

        lax.fori_loop(0, len(yhis), block, 0)


def partial_products(chunks, tile_blocks, tile_rows, tile_srcs, tile_count, near, across):
    slots, side = tile_blocks.shape[:2]
    columns = near.shape[1]
    smem = pl.BlockSpec(memory_space=pltpu.SMEM)
    vmem = pl.BlockSpec(memory_space=pltpu.VMEM)
    row_tiles = sum(len(yhis) for _, yhis in chunks)
    return pl.pallas_call(
        functools.partial(tiles_kernel, chunks),
        out_shape=[
            jax.ShapeDtypeStruct((len(yhis) * side, columns), jnp.bfloat16) for _, yhis in chunks
        ],
        in_specs=[smem, smem, smem, vmem, vmem, vmem],
        out_specs=[vmem] * len(chunks),
        scratch_shapes=[
            pltpu.SMEM((ROW_TILES,), jnp.int32),
            pltpu.SMEM((slots,), jnp.int32),
            pltpu.VMEM((side, columns), jnp.float32),
        ],
        compiler_params=pltpu.CompilerParams(vmem_limit_bytes=24 << 20),
        cost_estimate=pl.CostEstimate(
            flops=2 * row_tiles * side * side * columns,
            transcendentals=0,
            bytes_accessed=4 * row_tiles * side * columns,
        ),
        name="tile_products",
    )(tile_count, tile_rows, tile_srcs, tile_blocks, near, across)


def gather_panels(flow_cols):
    side = flow_cols.shape[0]
    own = jnp.concatenate([flow_cols, shifted(flow_cols, "ylo", 1)], 0)
    below1, above1 = shifted(own, "z", 1), shifted(own, "z", -1)
    below2, above2 = shifted(own, "z", 2), shifted(own, "z", -2)
    below3, above3 = shifted(below2, "z", 1), shifted(above2, "z", -1)
    below4, above4 = shifted(below2[:side], "z", 2), shifted(above2[side:], "z", -2)
    near = jnp.concatenate(
        [own, below1, above1, below2, above2, below3, above3, below4, above4], 0
    )
    return near, shifted(near, "core", 1)


def add(*terms):
    total = terms[0].astype(jnp.float32)
    for term in terms[1:]:
        total = total + term.astype(jnp.float32)
    return total.astype(jnp.bfloat16)


def reduce_along_x(products):
    every, half = range(N_YHI), N_YHI // 2
    up4, up3 = products([(4, every[:half]), (3, every)])
    down4, down3 = products([(4, every[half:]), (5, every)])
    up2, down2, up1, down1, own = products([(k, every) for k in (2, 6, 1, 7, 0)])
    up, down = shifted(up3, "x", 1), shifted(down3, "x", -1)
    up_far, down_far = shifted(up4, "x", 2), shifted(down4, "x", -2)
    rows = up4.shape[0]
    up = jnp.concatenate([add(up2[:rows], up[:rows], up_far), add(up2[rows:], up[rows:])], 0)
    down = jnp.concatenate(
        [add(down2[:rows], down[:rows]), add(down2[rows:], down[rows:], down_far)], 0
    )
    up, down = shifted(up, "x", 1), shifted(down, "x", -1)
    up, down = shifted(add(up1, up), "x", 1), shifted(add(down1, down), "x", -1)
    return add(own, up, down)


def body(flow_cols, restart, tile_blocks, tile_rows, tile_srcs, tile_count, dangling):
    side, columns = flow_cols.shape
    near, across = gather_panels(flow_cols)

    def products(chunks):
        return partial_products(
            chunks, tile_blocks, tile_rows, tile_srcs, tile_count, near, across
        )

    own_flow = flow_cols.astype(jnp.float32)
    mask_col = dangling.astype(jnp.float32)[:, None]
    constant = DAMP * (mask_col * own_flow) + (1.0 - DAMP) * restart.astype(jnp.float32)
    along_x, constant = lax.optimization_barrier((reduce_along_x(products), constant))
    shares = lax.all_to_all(along_x, "yhi", 0, 0, tiled=True).reshape(N_YHI, side, columns)
    summed = jnp.sum(shares.astype(jnp.float32), axis=0)
    return (DAMP * summed + constant).astype(jnp.bfloat16)


def solution(mesh):
    names = tuple(SIZES)
    fine = Mesh(mesh.devices.reshape(tuple(SIZES.values())), names)
    rows = P(names, None)
    in_specs = (rows, rows, P(names, None, None), P(names), P(names), P(names), P(names))
    return jax.shard_map(body, mesh=fine, in_specs=in_specs, out_specs=rows, check_vma=False)
```

```python
import functools

import jax
import jax.numpy as jnp
from jax import lax
from jax.experimental import pallas as pl
from jax.experimental.pallas import tpu as pltpu
from jax.sharding import Mesh, PartitionSpec as P

DAMP = 0.85
LOOP = (("ylo", 2), ("z", 8), ("core", 2))
LAYER = (("yhi", 4), ("x", 8))
SIZES = dict(LOOP + LAYER)
N_YLO, N_Z, N_CORE = SIZES["ylo"], SIZES["z"], SIZES["core"]
N_YHI, N_X = SIZES["yhi"], SIZES["x"]
ROW_TILES = N_YHI * N_X


def shifted(value, axis, by):
    size = SIZES[axis]
    return lax.ppermute(value, axis, [(i, (i + by) % size) for i in range(size)])


def sent_outward(value, by):
    pairs = [
        (core * N_X + x, core * N_X + (x + (by if core == 0 else -by)) % N_X)
        for core in range(N_CORE)
        for x in range(N_X)
    ]
    return lax.ppermute(value, ("core", "x"), pairs)


def tiles_kernel(chunks, count, rows, srcs, tiles, near, across, *refs):
    outs, (head, following, acc) = refs[: len(chunks)], refs[len(chunks) :]
    side = tiles.shape[1]
    my_ylo, my_z, my_core = lax.axis_index("ylo"), lax.axis_index("z"), lax.axis_index("core")
    my_x = lax.axis_index("x")

    def clear(r, carry):
        head[r] = -1
        return carry

    lax.fori_loop(0, ROW_TILES, clear, 0)

    def link(s, carry):
        r = rows[s]
        following[s] = head[r]
        head[r] = s
        return carry

    lax.fori_loop(0, count[0], link, 0)

    def add_product(s):
        src = srcs[s]
        dz = ((src // N_CORE) % N_Z + N_Z - my_z) % N_Z
        dy = (src // (N_CORE * N_Z) + N_YLO - my_ylo) % N_YLO
        slot = jnp.where(dz >= N_Z // 2, (N_Z - dz) * 2 - 1, 2 * dz)
        panel = pl.ds(pl.multiple_of((slot * N_YLO + dy) * side, side), side)
        same_core = src % N_CORE == my_core

        @pl.when(same_core)
        def _():
            acc[...] += jnp.dot(tiles[s], near[panel, :], preferred_element_type=jnp.float32)

        @pl.when(jnp.logical_not(same_core))
        def _():
            acc[...] += jnp.dot(tiles[s], across[panel, :], preferred_element_type=jnp.float32)

        return following[s]

    def chunk(out, base, k):
        x = (my_x + jnp.where(my_core == 0, k, -k) + N_X) % N_X

        def block(yhi, carry):
            first = head[yhi * N_X + x]
            where = pl.ds(pl.multiple_of((base + yhi) * side, side), side)

            @pl.when(first < 0)
            def _():
                out[where, :] = jnp.zeros((side, out.shape[1]), out.dtype)

            @pl.when(first >= 0)
            def _():
                acc[...] = jnp.zeros_like(acc)
                lax.while_loop(lambda s: s >= 0, add_product, first)
                out[where, :] = acc[...].astype(out.dtype)

            return carry

        lax.fori_loop(0, N_YHI, block, 0)

    for out, ks in zip(outs, chunks):
        for i, k in enumerate(ks):
            chunk(out, i * N_YHI, k)


def partial_products(chunks, tile_blocks, tile_rows, tile_srcs, tile_count, near, across):
    slots, side = tile_blocks.shape[:2]
    columns = near.shape[1]
    smem = pl.BlockSpec(memory_space=pltpu.SMEM)
    vmem = pl.BlockSpec(memory_space=pltpu.VMEM)
    row_tiles = N_YHI * sum(len(ks) for ks in chunks)
    return pl.pallas_call(
        functools.partial(tiles_kernel, chunks),
        out_shape=[
            jax.ShapeDtypeStruct((len(ks) * N_YHI * side, columns), jnp.bfloat16) for ks in chunks
        ],
        in_specs=[smem, smem, smem, vmem, vmem, vmem],
        out_specs=[vmem] * len(chunks),
        scratch_shapes=[
            pltpu.SMEM((ROW_TILES,), jnp.int32),
            pltpu.SMEM((slots,), jnp.int32),
            pltpu.VMEM((side, columns), jnp.float32),
        ],
        compiler_params=pltpu.CompilerParams(vmem_limit_bytes=24 << 20),
        cost_estimate=pl.CostEstimate(
            flops=2 * row_tiles * side * side * columns,
            transcendentals=0,
            bytes_accessed=4 * row_tiles * side * columns,
        ),
        name="tile_products",
    )(tile_count, tile_rows, tile_srcs, tile_blocks, near, across)


def gather_panels(flow_cols):
    side = flow_cols.shape[0]
    own = jnp.concatenate([flow_cols, shifted(flow_cols, "ylo", 1)], 0)
    below1, above1 = shifted(own, "z", 1), shifted(own, "z", -1)
    below2, above2 = shifted(own, "z", 2), shifted(own, "z", -2)
    below3, above3 = shifted(below2, "z", 1), shifted(above2, "z", -1)
    below4, above4 = shifted(below2[:side], "z", 2), shifted(above2[side:], "z", -2)
    near = jnp.concatenate(
        [own, below1, above1, below2, above2, below3, above3, below4, above4], 0
    )
    return near, shifted(near, "core", 1)


def add(*terms):
    total = terms[0].astype(jnp.float32)
    for term in terms[1:]:
        total = total + term.astype(jnp.float32)
    return total.astype(jnp.bfloat16)


def reduce_along_x(products):
    give3, keep4, keep3 = products([(-3,), (4,), (3,)])
    give21, keep2, keep1, own = products([(-2, -1), (2,), (1,), (0,)])
    chunk = own.shape[0]
    got3, got21 = shifted(give3, "core", 1), shifted(give21, "core", 1)
    other = sent_outward(got3, 1)
    mine = add(keep2, sent_outward(keep3, 1), sent_outward(keep4, 2))
    other = sent_outward(add(got21[:chunk], other), 1)
    mine = sent_outward(mine, 1)
    other = sent_outward(add(got21[chunk:], other), 1)
    mine = sent_outward(add(keep1, mine), 1)
    return add(own, mine, shifted(other, "core", 1))


def body(flow_cols, restart, tile_blocks, tile_rows, tile_srcs, tile_count, dangling):
    side, columns = flow_cols.shape
    near, across = gather_panels(flow_cols)

    def products(chunks):
        return partial_products(
            chunks, tile_blocks, tile_rows, tile_srcs, tile_count, near, across
        )

    own_flow = flow_cols.astype(jnp.float32)
    mask_col = dangling.astype(jnp.float32)[:, None]
    constant = DAMP * (mask_col * own_flow) + (1.0 - DAMP) * restart.astype(jnp.float32)
    along_x, constant = lax.optimization_barrier((reduce_along_x(products), constant))
    shares = lax.all_to_all(along_x, "yhi", 0, 0, tiled=True).reshape(N_YHI, side, columns)
    summed = jnp.sum(shares.astype(jnp.float32), axis=0)
    return (DAMP * summed + constant).astype(jnp.bfloat16)


def solution(mesh):
    names = tuple(SIZES)
    fine = Mesh(mesh.devices.reshape(tuple(SIZES.values())), names)
    rows = P(names, None)
    in_specs = (rows, rows, P(names, None, None), P(names), P(names), P(names), P(names))
    return jax.shard_map(body, mesh=fine, in_specs=in_specs, out_specs=rows, check_vma=False)
```

```python
import functools

import jax
import jax.numpy as jnp
from jax import lax
from jax.experimental import pallas as pl
from jax.experimental.pallas import tpu as pltpu
from jax.sharding import Mesh, PartitionSpec as P

DAMP = 0.85
LOOP = (("ylo", 2), ("z", 8), ("core", 2))
LAYER = (("yhi", 4), ("x", 8))
SIZES = dict(LOOP + LAYER)
N_YLO, N_Z, N_CORE = SIZES["ylo"], SIZES["z"], SIZES["core"]
N_YHI, N_X = SIZES["yhi"], SIZES["x"]
ROW_TILES = N_YHI * N_X


def shifted(value, axis, by):
    size = SIZES[axis]
    return lax.ppermute(value, axis, [(i, (i + by) % size) for i in range(size)])


def sent_outward(value, axis, by):
    size = SIZES[axis]
    names = tuple(name for name in SIZES if name in (axis, "core"))

    def index(core, place):
        return place * N_CORE + core if names[1] == "core" else core * size + place

    pairs = [
        (index(core, i), index(core, (i + (by if core == 0 else -by)) % size))
        for core in range(N_CORE)
        for i in range(size)
    ]
    return lax.ppermute(value, names, pairs)


def tiles_kernel(chunks, count, rows, srcs, tiles, panels, *refs):
    outs, (head, following, acc) = refs[: len(chunks)], refs[len(chunks) :]
    side = tiles.shape[1]
    my_ylo, my_z, my_core = lax.axis_index("ylo"), lax.axis_index("z"), lax.axis_index("core")
    my_x = lax.axis_index("x")

    def clear(r, carry):
        head[r] = -1
        return carry

    lax.fori_loop(0, ROW_TILES, clear, 0)

    def link(s, carry):
        r = rows[s]
        following[s] = head[r]
        head[r] = s
        return carry

    lax.fori_loop(0, count[0], link, 0)

    def product(s):
        place = panel_place(srcs[s], my_ylo, my_z, my_core)
        panel = pl.ds(pl.multiple_of(place * side, side), side)
        return jnp.dot(tiles[s], panels[panel, :], preferred_element_type=jnp.float32)

    def add_product(s):
        acc[...] += product(s)
        return following[s]

    def chunk(out, base, k):
        x = (my_x + jnp.where(my_core == 0, k, -k) + N_X) % N_X

        def block(yhi, carry):
            first = head[yhi * N_X + x]
            where = pl.ds(pl.multiple_of((base + yhi) * side, side), side)

            @pl.when(first < 0)
            def _():
                out[where, :] = jnp.zeros((side, out.shape[1]), out.dtype)

            @pl.when(first >= 0)
            def _():
                acc[...] = product(first)
                lax.while_loop(lambda s: s >= 0, add_product, following[first])
                out[where, :] = acc[...].astype(out.dtype)

            return carry

        lax.fori_loop(0, N_YHI, block, 0)

    for out, ks in zip(outs, chunks):
        for i, k in enumerate(ks):
            chunk(out, i * N_YHI, k)


def partial_products(chunks, tile_blocks, tile_rows, tile_srcs, tile_count, panels):
    slots, side = tile_blocks.shape[:2]
    columns = panels.shape[1]
    smem = pl.BlockSpec(memory_space=pltpu.SMEM)
    vmem = pl.BlockSpec(memory_space=pltpu.VMEM)
    row_tiles = N_YHI * sum(len(ks) for ks in chunks)
    return pl.pallas_call(
        functools.partial(tiles_kernel, chunks),
        out_shape=[
            jax.ShapeDtypeStruct((len(ks) * N_YHI * side, columns), jnp.bfloat16) for ks in chunks
        ],
        in_specs=[smem, smem, smem, vmem, vmem],
        out_specs=[vmem] * len(chunks),
        scratch_shapes=[
            pltpu.SMEM((ROW_TILES,), jnp.int32),
            pltpu.SMEM((slots,), jnp.int32),
            pltpu.VMEM((side, columns), jnp.float32),
        ],
        compiler_params=pltpu.CompilerParams(vmem_limit_bytes=24 << 20),
        cost_estimate=pl.CostEstimate(
            flops=2 * row_tiles * side * side * columns,
            transcendentals=0,
            bytes_accessed=4 * row_tiles * side * columns,
        ),
        name="tile_products",
    )(tile_count, tile_rows, tile_srcs, tile_blocks, panels)


def gather_panels(flow_cols):
    side = flow_cols.shape[0]
    pair = jnp.concatenate([flow_cols, shifted(flow_cols, "core", 1)], 0)
    far2, far1 = sent_outward(pair, "z", 2), sent_outward(pair, "z", 1)
    far3, far4 = sent_outward(far2, "z", 1), sent_outward(far2[:side], "z", 2)
    far12, far34 = jnp.concatenate([far1, far2], 0), jnp.concatenate([far3, far4], 0)
    first = [shifted(flow_cols, "ylo", 1), far12, shifted(far12, "ylo", 1)]
    second = [far34, shifted(far34, "ylo", 1)]
    swapped = [shifted(jnp.concatenate(part, 0), "core", 1) for part in (first, second)]
    return jnp.concatenate([pair] + first + second + swapped, 0)


def panel_place(src, my_ylo, my_z, my_core):
    off_ylo = (src // (N_CORE * N_Z) + N_YLO - my_ylo) % N_YLO
    off_z = (src // N_CORE % N_Z + N_Z - my_z) % N_Z
    off_core = (src % N_CORE + N_CORE - my_core) % N_CORE
    far = jnp.where(my_core == 0, (N_Z - off_z) % N_Z, off_z)
    half = N_Z // 2
    theirs = (
        ((far == 0) & (off_ylo + off_core == 2)) | ((far == half) & (off_core == 1)) | (far > half)
    )
    far = jnp.where(theirs, (N_Z - far) % N_Z, far)
    off_core = jnp.where(theirs, 1 - off_core, off_core)
    place = jnp.where(
        far == 0,
        jnp.where(off_ylo == 0, off_core, 2),
        jnp.where(
            far <= 2,
            1 + 2 * far + off_core + 4 * off_ylo,
            jnp.where(far == 3, 11 + off_core, 13) + 3 * off_ylo,
        ),
    )
    return place + jnp.where(theirs, 15, 0)


def add(*terms):
    total = terms[0].astype(jnp.float32)
    for term in terms[1:]:
        total = total + term.astype(jnp.float32)
    return total.astype(jnp.bfloat16)


def reduce_along_x(products):
    give, keep4, keep3, keep2, keep1, own = products
    chunk = own.shape[0]
    got = shifted(give, "core", 1)
    got3, got2, got1 = (got[i * chunk : (i + 1) * chunk] for i in range(3))
    other, mine = sent_outward(got3, "x", 1), sent_outward(keep3, "x", 1)
    mine = add(keep2, mine, sent_outward(keep4, "x", 2))
    other = sent_outward(add(got2, other), "x", 1)
    mine = sent_outward(mine, "x", 1)
    other = sent_outward(add(got1, other), "x", 1)
    mine = sent_outward(add(keep1, mine), "x", 1)
    return add(own, mine, shifted(other, "core", 1))


def body(flow_cols, restart, tile_blocks, tile_rows, tile_srcs, tile_count, dangling):
    side, columns = flow_cols.shape
    panels = gather_panels(flow_cols)

    products = partial_products(
        [(-3, -2, -1), (4,), (3,), (2,), (1,), (0,)],
        tile_blocks,
        tile_rows,
        tile_srcs,
        tile_count,
        panels,
    )
    own_flow = flow_cols.astype(jnp.float32)
    mask_col = dangling.astype(jnp.float32)[:, None]
    constant = DAMP * (mask_col * own_flow) + (1.0 - DAMP) * restart.astype(jnp.float32)
    along_x, constant = lax.optimization_barrier((reduce_along_x(products), constant))
    shares = lax.all_to_all(along_x, "yhi", 0, 0, tiled=True).reshape(N_YHI, side, columns)
    summed = jnp.sum(shares.astype(jnp.float32), axis=0)
    return (DAMP * summed + constant).astype(jnp.bfloat16)


def solution(mesh):
    names = tuple(SIZES)
    fine = Mesh(mesh.devices.reshape(tuple(SIZES.values())), names)
    rows = P(names, None)
    in_specs = (rows, rows, P(names, None, None), P(names), P(names), P(names), P(names))
    return jax.shard_map(body, mesh=fine, in_specs=in_specs, out_specs=rows, check_vma=False)
```

```python
import functools

import jax
import jax.numpy as jnp
from jax import lax
from jax.experimental import pallas as pl
from jax.experimental.pallas import tpu as pltpu
from jax.sharding import Mesh, PartitionSpec as P

DAMP = 0.85
LOOP = (("ylo", 2), ("z", 8), ("core", 2))
LAYER = (("yhi", 4), ("x", 8))
SIZES = dict(LOOP + LAYER)
N_YLO, N_Z, N_CORE = SIZES["ylo"], SIZES["z"], SIZES["core"]
N_YHI, N_X = SIZES["yhi"], SIZES["x"]
ROW_TILES = N_YHI * N_X


def shifted(value, axis, by):
    size = SIZES[axis]
    return lax.ppermute(value, axis, [(i, (i + by) % size) for i in range(size)])


def sent_outward(value, axis, by):
    size = SIZES[axis]
    names = tuple(name for name in SIZES if name in (axis, "core"))

    def index(core, place):
        return place * N_CORE + core if names[1] == "core" else core * size + place

    pairs = [
        (index(core, i), index(core, (i + (by if core == 0 else -by)) % size))
        for core in range(N_CORE)
        for i in range(size)
    ]
    return lax.ppermute(value, names, pairs)


def tiles_kernel(chunks, count, rows, srcs, tiles, panels, *refs):
    outs, (head, following, acc) = refs[: len(chunks)], refs[len(chunks) :]
    side = tiles.shape[1]
    my_ylo, my_z, my_core = lax.axis_index("ylo"), lax.axis_index("z"), lax.axis_index("core")
    my_x = lax.axis_index("x")

    def clear(r, carry):
        head[r] = -1
        return carry

    lax.fori_loop(0, ROW_TILES, clear, 0)

    def link(s, carry):
        r = rows[s]
        following[s] = head[r]
        head[r] = s
        return carry

    lax.fori_loop(0, count[0], link, 0)

    def product(s):
        place = panel_place(srcs[s], my_ylo, my_z, my_core)
        panel = pl.ds(pl.multiple_of(place * side, side), side)
        return jnp.dot(tiles[s], panels[panel, :], preferred_element_type=jnp.float32)

    def add_product(s):
        acc[...] += product(s)
        return following[s]

    def chunk(out, base, k):
        x = (my_x + jnp.where(my_core == 0, k, -k) + N_X) % N_X

        def block(yhi, carry):
            first = head[yhi * N_X + x]
            where = pl.ds(pl.multiple_of((base + yhi) * side, side), side)

            @pl.when(first < 0)
            def _():
                out[where, :] = jnp.zeros((side, out.shape[1]), out.dtype)

            @pl.when(first >= 0)
            def _():
                acc[...] = product(first)
                lax.while_loop(lambda s: s >= 0, add_product, following[first])
                out[where, :] = acc[...].astype(out.dtype)

            return carry

        lax.fori_loop(0, N_YHI, block, 0)

    for out, ks in zip(outs, chunks):
        for i, k in enumerate(ks):
            chunk(out, i * N_YHI, k)


def partial_products(chunks, tile_blocks, tile_rows, tile_srcs, tile_count, panels):
    slots, side = tile_blocks.shape[:2]
    columns = panels.shape[1]
    smem = pl.BlockSpec(memory_space=pltpu.SMEM)
    vmem = pl.BlockSpec(memory_space=pltpu.VMEM)
    row_tiles = N_YHI * sum(len(ks) for ks in chunks)
    return pl.pallas_call(
        functools.partial(tiles_kernel, chunks),
        out_shape=[
            jax.ShapeDtypeStruct((len(ks) * N_YHI * side, columns), jnp.bfloat16) for ks in chunks
        ],
        in_specs=[smem, smem, smem, vmem, vmem],
        out_specs=[vmem] * len(chunks),
        scratch_shapes=[
            pltpu.SMEM((ROW_TILES,), jnp.int32),
            pltpu.SMEM((slots,), jnp.int32),
            pltpu.VMEM((side, columns), jnp.float32),
        ],
        compiler_params=pltpu.CompilerParams(vmem_limit_bytes=24 << 20),
        cost_estimate=pl.CostEstimate(
            flops=2 * row_tiles * side * side * columns,
            transcendentals=0,
            bytes_accessed=4 * row_tiles * side * columns,
        ),
        name="tile_products",
    )(tile_count, tile_rows, tile_srcs, tile_blocks, panels)


def gather_panels(flow_cols):
    side = flow_cols.shape[0]
    own = jnp.concatenate([flow_cols, shifted(flow_cols, "ylo", 1)], 0)
    below1, above1 = shifted(own, "z", 1), shifted(own, "z", -1)
    below2, above2 = shifted(own, "z", 2), shifted(own, "z", -2)
    below3, above3 = shifted(below2, "z", 1), shifted(above2, "z", -1)
    below4, above4 = shifted(below2[:side], "z", 2), shifted(above2[side:], "z", -2)
    near = jnp.concatenate(
        [own, below1, above1, below2, above2, below3, above3, below4, above4], 0
    )
    return jnp.concatenate([near, shifted(near, "core", 1)], 0)


def panel_place(src, my_ylo, my_z, my_core):
    off_ylo = (src // (N_CORE * N_Z) + N_YLO - my_ylo) % N_YLO
    off_z = (src // N_CORE % N_Z + N_Z - my_z) % N_Z
    off_core = (src % N_CORE + N_CORE - my_core) % N_CORE
    slot = jnp.where(off_z >= N_Z // 2, (N_Z - off_z) * 2 - 1, 2 * off_z)
    return (off_core * N_Z + slot) * N_YLO + off_ylo


def add(*terms):
    total = terms[0].astype(jnp.float32)
    for term in terms[1:]:
        total = total + term.astype(jnp.float32)
    return total.astype(jnp.bfloat16)


def reduce_along_x(products):
    (keep4,) = products([(4,)])
    give, keep3, keep2, keep1, own = products([(-3, -2, -1), (3,), (2,), (1,), (0,)])
    chunk = own.shape[0]
    mine = sent_outward(keep4, "x", 1)
    got = shifted(give, "core", 1)
    got3, got2, got1 = (got[i * chunk : (i + 1) * chunk] for i in range(3))
    other = sent_outward(got3, "x", 1)
    mine = sent_outward(add(keep3, mine), "x", 1)
    other = sent_outward(add(got2, other), "x", 1)
    mine = sent_outward(add(keep2, mine), "x", 1)
    other = sent_outward(add(got1, other), "x", 1)
    mine = sent_outward(add(keep1, mine), "x", 1)
    return add(own, mine, shifted(other, "core", 1))


def body(flow_cols, restart, tile_blocks, tile_rows, tile_srcs, tile_count, dangling):
    side, columns = flow_cols.shape
    panels = gather_panels(flow_cols)

    def products(chunks):
        return partial_products(chunks, tile_blocks, tile_rows, tile_srcs, tile_count, panels)

    own_flow = flow_cols.astype(jnp.float32)
    mask_col = dangling.astype(jnp.float32)[:, None]
    constant = DAMP * (mask_col * own_flow) + (1.0 - DAMP) * restart.astype(jnp.float32)
    along_x, constant = lax.optimization_barrier((reduce_along_x(products), constant))
    shares = lax.all_to_all(along_x, "yhi", 0, 0, tiled=True).reshape(N_YHI, side, columns)
    summed = jnp.sum(shares.astype(jnp.float32), axis=0)
    return (DAMP * summed + constant).astype(jnp.bfloat16)


def solution(mesh):
    names = tuple(SIZES)
    fine = Mesh(mesh.devices.reshape(tuple(SIZES.values())), names)
    rows = P(names, None)
    in_specs = (rows, rows, P(names, None, None), P(names), P(names), P(names), P(names))
    return jax.shard_map(body, mesh=fine, in_specs=in_specs, out_specs=rows, check_vma=False)
```

```python
import functools

import jax
import jax.numpy as jnp
from jax import lax
from jax.experimental import pallas as pl
from jax.experimental.pallas import tpu as pltpu
from jax.sharding import Mesh, PartitionSpec as P

DAMP = 0.85
LOOP = (("ylo", 2), ("z", 8), ("core", 2))
LAYER = (("yhi", 4), ("x", 8))
SIZES = dict(LOOP + LAYER)
N_YLO, N_Z, N_CORE = SIZES["ylo"], SIZES["z"], SIZES["core"]
N_YHI, N_X = SIZES["yhi"], SIZES["x"]
ROW_TILES = N_YHI * N_X


def shifted(value, axis, by):
    size = SIZES[axis]
    return lax.ppermute(value, axis, [(i, (i + by) % size) for i in range(size)])


def sent_outward(value, axis, by):
    size = SIZES[axis]
    names = tuple(name for name in SIZES if name in (axis, "core"))

    def index(core, place):
        return place * N_CORE + core if names[1] == "core" else core * size + place

    pairs = [
        (index(core, i), index(core, (i + (by if core == 0 else -by)) % size))
        for core in range(N_CORE)
        for i in range(size)
    ]
    return lax.ppermute(value, names, pairs)


def tiles_kernel(chunks, count, rows, srcs, tiles, near, across, *refs):
    outs, (head, following, acc) = refs[: len(chunks)], refs[len(chunks) :]
    side = tiles.shape[1]
    my_ylo, my_z, my_core = lax.axis_index("ylo"), lax.axis_index("z"), lax.axis_index("core")
    my_x = lax.axis_index("x")

    def clear(r, carry):
        head[r] = -1
        return carry

    lax.fori_loop(0, ROW_TILES, clear, 0)

    def link(s, carry):
        r = rows[s]
        following[s] = head[r]
        head[r] = s
        return carry

    lax.fori_loop(0, count[0], link, 0)

    def add_product(s):
        same_core, place = panel_place(srcs[s], my_ylo, my_z, my_core)
        panel = pl.ds(pl.multiple_of(place * side, side), side)

        @pl.when(same_core)
        def _():
            acc[...] += jnp.dot(tiles[s], near[panel, :], preferred_element_type=jnp.float32)

        @pl.when(jnp.logical_not(same_core))
        def _():
            acc[...] += jnp.dot(tiles[s], across[panel, :], preferred_element_type=jnp.float32)

        return following[s]

    def chunk(out, base, k):
        x = (my_x + jnp.where(my_core == 0, k, -k) + N_X) % N_X

        def block(yhi, carry):
            first = head[yhi * N_X + x]
            where = pl.ds(pl.multiple_of((base + yhi) * side, side), side)

            @pl.when(first < 0)
            def _():
                out[where, :] = jnp.zeros((side, out.shape[1]), out.dtype)

            @pl.when(first >= 0)
            def _():
                acc[...] = jnp.zeros_like(acc)
                lax.while_loop(lambda s: s >= 0, add_product, first)
                out[where, :] = acc[...].astype(out.dtype)

            return carry

        lax.fori_loop(0, N_YHI, block, 0)

    for out, ks in zip(outs, chunks):
        for i, k in enumerate(ks):
            chunk(out, i * N_YHI, k)


def partial_products(chunks, tile_blocks, tile_rows, tile_srcs, tile_count, near, across):
    slots, side = tile_blocks.shape[:2]
    columns = near.shape[1]
    smem = pl.BlockSpec(memory_space=pltpu.SMEM)
    vmem = pl.BlockSpec(memory_space=pltpu.VMEM)
    row_tiles = N_YHI * sum(len(ks) for ks in chunks)
    return pl.pallas_call(
        functools.partial(tiles_kernel, chunks),
        out_shape=[
            jax.ShapeDtypeStruct((len(ks) * N_YHI * side, columns), jnp.bfloat16) for ks in chunks
        ],
        in_specs=[smem, smem, smem, vmem, vmem, vmem],
        out_specs=[vmem] * len(chunks),
        scratch_shapes=[
            pltpu.SMEM((ROW_TILES,), jnp.int32),
            pltpu.SMEM((slots,), jnp.int32),
            pltpu.VMEM((side, columns), jnp.float32),
        ],
        compiler_params=pltpu.CompilerParams(vmem_limit_bytes=24 << 20),
        cost_estimate=pl.CostEstimate(
            flops=2 * row_tiles * side * side * columns,
            transcendentals=0,
            bytes_accessed=4 * row_tiles * side * columns,
        ),
        name="tile_products",
    )(tile_count, tile_rows, tile_srcs, tile_blocks, near, across)


def gather_panels(flow_cols):
    side = flow_cols.shape[0]
    own = jnp.concatenate([flow_cols, shifted(flow_cols, "ylo", 1)], 0)
    below1, above1 = shifted(own, "z", 1), shifted(own, "z", -1)
    below2, above2 = shifted(own, "z", 2), shifted(own, "z", -2)
    below3, above3 = shifted(below2, "z", 1), shifted(above2, "z", -1)
    below4, above4 = shifted(below2[:side], "z", 2), shifted(above2[side:], "z", -2)
    near = jnp.concatenate(
        [own, below1, above1, below2, above2, below3, above3, below4, above4], 0
    )
    return near, shifted(near, "core", 1)


def panel_place(src, my_ylo, my_z, my_core):
    off_ylo = (src // (N_CORE * N_Z) + N_YLO - my_ylo) % N_YLO
    off_z = (src // N_CORE % N_Z + N_Z - my_z) % N_Z
    off_core = (src % N_CORE + N_CORE - my_core) % N_CORE
    slot = jnp.where(off_z >= N_Z // 2, (N_Z - off_z) * 2 - 1, 2 * off_z)
    return off_core == 0, slot * N_YLO + off_ylo


def add(*terms):
    total = terms[0].astype(jnp.float32)
    for term in terms[1:]:
        total = total + term.astype(jnp.float32)
    return total.astype(jnp.bfloat16)


def reduce_along_x(products):
    (keep4,) = products([(4,)])
    give, keep3, keep2, keep1, own = products([(-3, -2, -1), (3,), (2,), (1,), (0,)])
    chunk = own.shape[0]
    mine = sent_outward(keep4, "x", 1)
    got = shifted(give, "core", 1)
    got3, got2, got1 = (got[i * chunk : (i + 1) * chunk] for i in range(3))
    other = sent_outward(got3, "x", 1)
    mine = sent_outward(add(keep3, mine), "x", 1)
    other = sent_outward(add(got2, other), "x", 1)
    mine = sent_outward(add(keep2, mine), "x", 1)
    other = sent_outward(add(got1, other), "x", 1)
    mine = sent_outward(add(keep1, mine), "x", 1)
    return add(own, mine, shifted(other, "core", 1))


def body(flow_cols, restart, tile_blocks, tile_rows, tile_srcs, tile_count, dangling):
    side, columns = flow_cols.shape
    near, across = gather_panels(flow_cols)

    def products(chunks):
        return partial_products(
            chunks, tile_blocks, tile_rows, tile_srcs, tile_count, near, across
        )

    own_flow = flow_cols.astype(jnp.float32)
    mask_col = dangling.astype(jnp.float32)[:, None]
    constant = DAMP * (mask_col * own_flow) + (1.0 - DAMP) * restart.astype(jnp.float32)
    along_x, constant = lax.optimization_barrier((reduce_along_x(products), constant))
    shares = lax.all_to_all(along_x, "yhi", 0, 0, tiled=True).reshape(N_YHI, side, columns)
    summed = jnp.sum(shares.astype(jnp.float32), axis=0)
    return (DAMP * summed + constant).astype(jnp.bfloat16)


def solution(mesh):
    names = tuple(SIZES)
    fine = Mesh(mesh.devices.reshape(tuple(SIZES.values())), names)
    rows = P(names, None)
    in_specs = (rows, rows, P(names, None, None), P(names), P(names), P(names), P(names))
    return jax.shard_map(body, mesh=fine, in_specs=in_specs, out_specs=rows, check_vma=False)
```
